32 devices in a mesh: gx: 8 (over z, core), gy: 4 (over y, x).
Axes of the slice: x: 2, y: 2, z: 4, core: 2. Of those that a mesh axis runs over, the one named last changes fastest.
Arguments:
- points: bfloat16 [64, 65536], P(None, ('gx', 'gy')), may hold values from -6 to 6
- vectors: bfloat16 [32, 65536], P(None, ('gx', 'gy')), may hold values from -6 to 6
- leaf_pick: int32 [128, 128], P(('gx', 'gy')), may hold values from 0 to 511
- leaf_assign: int32 [128, 512], P(('gx', 'gy')), may hold values from 0 to 127
- device_pick: int32 [32, 128], P(('gx', 'gy')), may hold values from 0 to 511
- device_assign: int32 [32, 512], P(('gx', 'gy')), may hold values from 0 to 127
- node_pick: int32 [8, 3, 128], P('gx'), may hold values from 0 to 255
- node_assign: int32 [8, 3, 256], P('gx'), may hold values from 0 to 127
- far_mask: int32 [8, 8], P('gx'), may hold values from 0 to 1, as said below
- near_lower: int32 [32, 4, 12], P(('gx', 'gy')), may hold values from -1 to 3, as said below
- near_upper: int32 [32, 4, 12], P(('gx', 'gy')), may hold values from 0 to 3, as said below
Outputs:
- potential: float32 [32, 65536], P(None, ('gx', 'gy'))
The draws below stay inside these ranges and needn't reach their ends.
Inputs may be any that keep to these rules, and one draw needn't show every extreme that they name: near_lower[d, o, j] is a local leaf of device d forming a near pair with local leaf near_upper[d, o, j] of device d + o + 1, or -1 for an empty slot; the slots of one d and o never name the same pair of leaves, and no live slot names a device past the last. `near_upper`: A local leaf of device d + o + 1, read only where near_lower is live. `far_mask`: Symmetric, zero on the diagonal, one where the two group indices differ by exactly 1.
All inputs are finite; a program needn't handle non-finite values.
Results may differ from the reference program's by a relative error of at most 0.0015.
Values may be sent and summed in bfloat16 or wider, within the bound.
No kernel may reach another device: no remote copies, remote signals or barrier semaphores. Data moves between devices by JAX's collectives and lax.ppermute only.
A program may use at most 128 MiB of HBM per device.

```python
import jax
import jax.numpy as jnp
from jax import lax

DIM = 64
COLS = 32
LEAF = 512
SKEL = 128
LPD = 4
SLOTS = 12
REACH = 4
LEAVES = 128
NPTS = 65536
N_GX = 8
N_GY = 4
DEVICES = 32


def leaf_codes(row_key):
    return jax.random.permutation(row_key, LPD * LPD)[:SLOTS].astype(jnp.int32)


def near_draw(key):
    near_key = jax.random.fold_in(key, 7)
    row_keys = jax.random.split(jax.random.fold_in(near_key, 1), DEVICES * REACH)
    pair_codes = jax.vmap(leaf_codes)(row_keys).reshape(DEVICES, REACH, SLOTS)
    powers = jax.random.randint(jax.random.fold_in(near_key, 2), (DEVICES,), 1, 5)
    weights = jnp.left_shift(jnp.ones_like(powers), powers)
    slot_rolls = jax.random.randint(jax.random.fold_in(near_key, 3), (DEVICES, REACH, SLOTS), 0, 8)
    device_ids = jnp.arange(DEVICES, dtype=jnp.int32)[:, None, None]
    offsets = jnp.arange(1, REACH + 1, dtype=jnp.int32)[None, :, None]
    live_slots = (slot_rolls < weights[:, None, None]) & (device_ids + offsets < DEVICES)
    lower_leaf = jnp.where(live_slots, pair_codes // LPD, -1).astype(jnp.int32)
    upper_leaf = (pair_codes % LPD).astype(jnp.int32)
    return (lower_leaf, upper_leaf)


def draw_near_lower(key, part):
    return near_draw(key)[0]


def draw_near_upper(key, part):
    return near_draw(key)[1]


def draw_far_mask(key, part):
    coin_flips = jax.random.randint(jax.random.fold_in(key, 21), (N_GX, N_GX), 0, 2)
    row_ids = jnp.arange(N_GX, dtype=jnp.int32)[:, None]
    col_ids = jnp.arange(N_GX, dtype=jnp.int32)[None, :]
    symmetric = jnp.where(row_ids < col_ids, coin_flips, coin_flips.T)
    distance = jnp.abs(row_ids - col_ids)
    flagged = jnp.where(distance == 1, 1, symmetric)
    return jnp.where(distance >= 1, flagged, 0).astype(jnp.int32)


def touch_ends(drawn, own_key, smallest, largest):
    shape = drawn.shape
    spot = [jax.random.randint(jax.random.fold_in(own_key, axis), (), 0, shape[axis]) for axis in range(len(shape))]
    drawn = drawn.at[tuple(spot)].set(smallest)
    longest = shape.index(max(shape))
    spot[longest] = (spot[longest] + 1) % shape[longest]
    return drawn.at[tuple(spot)].set(largest)


def level_of(key, extent, cuts, low, largest):
    gain = 1.0
    for dim, parts in cuts:
        heights = jax.random.uniform(jax.random.fold_in(jax.random.fold_in(key, 6), dim), (parts,), jnp.float32, low / len(cuts), largest / len(cuts))
        gain = gain * jnp.repeat(jnp.exp(heights), extent[dim] // parts).reshape((-1,) + (1,) * (len(extent) - 1 - dim))
    return gain


def centred(own_key, shape, width, bound, pieces=(), kind=jnp.bfloat16):
    gain = level_of(own_key, shape, pieces, -0.22, 0.18) if pieces else 1.0
    values = jax.random.normal(own_key, shape, jnp.float32) * width * gain
    return jnp.minimum(jnp.maximum(values, -bound), bound).astype(kind)


def setup_inputs(seed: int = 0) -> dict:
    seeds = jax.random.split(jax.random.key(seed), 12)
    return {
        "points": centred(seeds[0], (DIM, NPTS), 1.0, 6.0, ((1, 32),)),
        "vectors": centred(seeds[1], (COLS, NPTS), 1.0, 6.0, ((1, 32),)),
        "leaf_pick": touch_ends(jax.random.randint(seeds[2], (LEAVES, SKEL), 0, LEAF), jax.random.fold_in(seeds[2], 1), 0, LEAF - 1).astype(jnp.int32),
        "leaf_assign": touch_ends(jax.random.randint(seeds[3], (LEAVES, LEAF), 0, SKEL), jax.random.fold_in(seeds[3], 1), 0, SKEL - 1).astype(jnp.int32),
        "device_pick": touch_ends(jax.random.randint(seeds[4], (DEVICES, SKEL), 0, LPD * SKEL), jax.random.fold_in(seeds[4], 1), 0, (LPD * SKEL) - 1).astype(jnp.int32),
        "device_assign": touch_ends(jax.random.randint(seeds[5], (DEVICES, LPD * SKEL), 0, SKEL), jax.random.fold_in(seeds[5], 1), 0, SKEL - 1).astype(jnp.int32),
        "node_pick": touch_ends(jax.random.randint(seeds[6], (N_GX, N_GY - 1, SKEL), 0, 2 * SKEL), jax.random.fold_in(seeds[6], 1), 0, (2 * SKEL) - 1).astype(jnp.int32),
        "node_assign": touch_ends(jax.random.randint(seeds[7], (N_GX, N_GY - 1, 2 * SKEL), 0, SKEL), jax.random.fold_in(seeds[7], 1), 0, SKEL - 1).astype(jnp.int32),
        "far_mask": draw_far_mask(jax.random.fold_in(seeds[11], 71), 0),
        "near_lower": draw_near_lower(jax.random.fold_in(seeds[11], 71), 0),
        "near_upper": draw_near_upper(jax.random.fold_in(seeds[11], 71), 0),
    }


KERNEL_RATE = 2.0


def kernel_block(source, target):
    decay_rate = KERNEL_RATE / source.shape[0]
    source_wide = source.astype(jnp.float32)
    target_wide = target.astype(jnp.float32)
    source_norm = jnp.sum(source_wide * source_wide, axis=0)
    target_norm = jnp.sum(target_wide * target_wide, axis=0)
    products = lax.dot_general(source, target, (((0,), (0,)), ((), ())), preferred_element_type=jnp.float32)
    return jnp.exp(-decay_rate * (source_norm[:, None] + target_norm[None, :] - 2.0 * products))


def add_columns(running, terms, first_col):
    first_col = jnp.asarray(first_col).astype(jnp.int32)
    current = lax.dynamic_slice_in_dim(running, first_col, terms.shape[1], 1)
    return lax.dynamic_update_slice_in_dim(running, current + terms, first_col, 1)


def pick_columns(table_matrix, col_index):
    return jnp.take(table_matrix, col_index, axis=1)


def sum_skeleton(weights, assignment):
    return jax.ops.segment_sum(weights.T, assignment, num_segments=SKEL).T


def near_field(points, columns, near_lower, near_upper):
    device_cols = LPD * LEAF
    start_terms = jnp.zeros((COLS, points.shape[1]), jnp.float32)

    def per_device(device, running):
        device = jnp.asarray(device).astype(jnp.int32)
        first_col = device * device_cols
        device_points = lax.dynamic_slice_in_dim(points, first_col, device_cols, 1)
        device_values = lax.dynamic_slice_in_dim(columns, first_col, device_cols, 1)

        def per_target(target, inner_terms):
            target_col = jnp.asarray(target).astype(jnp.int32) * LEAF
            target_points = lax.dynamic_slice_in_dim(device_points, target_col, LEAF, 1)
            kernel_tile = kernel_block(device_points, target_points).astype(jnp.bfloat16)
            self_terms = jnp.dot(device_values, kernel_tile, preferred_element_type=jnp.float32)
            return add_columns(inner_terms, self_terms, first_col + target_col)

        running = lax.fori_loop(0, LPD, per_target, running)

        def per_pair(pair_index, inner_terms):
            pair_index = jnp.asarray(pair_index).astype(jnp.int32)
            offset = pair_index // SLOTS
            slot_index = pair_index % SLOTS
            lower_leaf = near_lower[device, offset, slot_index].astype(jnp.int32)
            upper_leaf = near_upper[device, offset, slot_index].astype(jnp.int32)
            live_scale = (lower_leaf >= 0).astype(jnp.float32)
            lower_col = first_col + jnp.maximum(lower_leaf, 0) * LEAF
            upper_col = jnp.minimum((device + offset + 1) * device_cols + upper_leaf * LEAF, points.shape[1] - LEAF)
            low_points = lax.dynamic_slice_in_dim(points, lower_col, LEAF, 1)
            low_values = lax.dynamic_slice_in_dim(columns, lower_col, LEAF, 1)
            high_points = lax.dynamic_slice_in_dim(points, upper_col, LEAF, 1)
            high_values = lax.dynamic_slice_in_dim(columns, upper_col, LEAF, 1)
            kernel_tile = kernel_block(low_points, high_points).astype(jnp.bfloat16)
            to_upper = live_scale * jnp.dot(low_values, kernel_tile, preferred_element_type=jnp.float32)
            to_lower = live_scale * lax.dot_general(high_values, kernel_tile, (((1,), (1,)), ((), ())), preferred_element_type=jnp.float32)
            inner_terms = add_columns(inner_terms, to_lower, lower_col)
            return add_columns(inner_terms, to_upper, upper_col)

        return lax.fori_loop(0, REACH * SLOTS, per_pair, running)

    return lax.fori_loop(0, DEVICES, per_device, start_terms)


def far_field(points, columns, leaf_pick, leaf_assign, device_pick, device_assign, node_pick, node_assign, far_mask):
    leaves = LPD * DEVICES
    leaf_points = points.reshape(DIM, leaves, LEAF)
    leaf_values = columns.reshape(COLS, leaves, LEAF).astype(jnp.float32)
    skeleton_points = jax.vmap(pick_columns, in_axes=(1, 0))(leaf_points, leaf_pick)
    skeleton_weights = jax.vmap(sum_skeleton, in_axes=(1, 0))(leaf_values, leaf_assign)
    joined_points = skeleton_points.reshape(DEVICES, LPD, DIM, SKEL).transpose(0, 2, 1, 3).reshape(DEVICES, DIM, LPD * SKEL)
    joined_weights = skeleton_weights.reshape(DEVICES, LPD, COLS, SKEL).transpose(0, 2, 1, 3).reshape(DEVICES, COLS, LPD * SKEL)
    node_points = jax.vmap(pick_columns)(joined_points, device_pick).reshape(N_GX, N_GY, DIM, SKEL)
    node_weights = jax.vmap(sum_skeleton)(joined_weights, device_assign).reshape(N_GX, N_GY, COLS, SKEL)
    levels = N_GY.bit_length() - 1
    for level_index in range(1, levels + 1):
        node_count = N_GY >> level_index
        pair_points = node_points.reshape(N_GX, node_count, 2, DIM, SKEL).transpose(0, 1, 3, 2, 4).reshape(N_GX * node_count, DIM, 2 * SKEL)
        pair_weights = node_weights.reshape(N_GX, node_count, 2, COLS, SKEL).transpose(0, 1, 3, 2, 4).reshape(N_GX * node_count, COLS, 2 * SKEL)
        picks = node_pick[:, node_count - 1:2 * node_count - 1].reshape(N_GX * node_count, SKEL)
        assignments = node_assign[:, node_count - 1:2 * node_count - 1].reshape(N_GX * node_count, 2 * SKEL)
        node_points = jax.vmap(pick_columns)(pair_points, picks).reshape(N_GX, node_count, DIM, SKEL)
        node_weights = jax.vmap(sum_skeleton)(pair_weights, assignments).reshape(N_GX, node_count, COLS, SKEL)
    root_points = node_points[:, 0]
    root_weights = node_weights[:, 0]

    def kernels_from(source_root):
        return jax.vmap(kernel_block, in_axes=(None, 0))(source_root, root_points)

    root_kernels = jax.vmap(kernels_from)(root_points)
    far_flags = far_mask.astype(jnp.float32)
    root_potential = jnp.einsum("gh,hcs,hgst->gct", far_flags, root_weights, root_kernels, precision=lax.Precision.HIGHEST)
    node_potential = root_potential[:, None]
    for level_index in range(levels, 0, -1):
        node_count = N_GY >> level_index
        assignments = node_assign[:, node_count - 1:2 * node_count - 1].reshape(N_GX * node_count, 2 * SKEL)
        child_potential = jax.vmap(pick_columns)(node_potential.reshape(N_GX * node_count, COLS, SKEL), assignments)
        node_potential = child_potential.reshape(N_GX, node_count, COLS, 2, SKEL).transpose(0, 1, 3, 2, 4).reshape(N_GX, 2 * node_count, COLS, SKEL)
    device_potential = node_potential.reshape(DEVICES, COLS, SKEL)
    leaf_joined = jax.vmap(pick_columns)(device_potential, device_assign)
    leaf_potential = leaf_joined.reshape(DEVICES, COLS, LPD, SKEL).transpose(0, 2, 1, 3).reshape(leaves, COLS, SKEL)
    point_potential = jax.vmap(pick_columns)(leaf_potential, leaf_assign)
    return point_potential.transpose(1, 0, 2).reshape(COLS, leaves * LEAF)


def reference(points, vectors, leaf_pick, leaf_assign, device_pick, device_assign, node_pick, node_assign, far_mask, near_lower, near_upper):
    near_terms = near_field(points, vectors, near_lower, near_upper)
    far_terms = far_field(points, vectors, leaf_pick, leaf_assign, device_pick, device_assign, node_pick, node_assign, far_mask)
    return near_terms + far_terms
```

```python
import functools
import math

import jax
import jax.numpy as jnp
from jax import lax
from jax.experimental import pallas as pl
from jax.experimental.pallas import tpu as pltpu
from jax.sharding import PartitionSpec as P

LPD = 4
SKEL = 128
KERNEL_RATE = 2.0
LOG2E = math.log2(math.e)
ROWS_AUG = 16
F32, BF16 = jnp.float32, jnp.bfloat16
VMEM = pl.BlockSpec(memory_space=pltpu.VMEM)
SMEM = pl.BlockSpec(memory_space=pltpu.SMEM)


def passed_along(value, axis, steps):
    count = lax.axis_size(axis)
    first, last = (max(0, -steps), min(count, count - steps))
    return lax.ppermute(value, axis, [(source, source + steps) for source in range(first, last)])


def swapped(value, axis, mask):
    pairs = [(source, source ^ mask) for source in range(lax.axis_size(axis))]
    return lax.ppermute(value, axis, pairs)


def split3(value):
    first = value.astype(BF16)
    rest = value - first.astype(F32)
    second = rest.astype(BF16)
    third = (rest - second.astype(F32)).astype(BF16)
    return first, second, third


def norm_rows(points, scale, norms_first):
    wide = points.astype(F32)
    norm = -0.5 * scale * jnp.sum(wide * wide, axis=0, keepdims=True)
    row = lax.broadcasted_iota(jnp.int32, (ROWS_AUG, points.shape[1]), 0)
    start = 0 if norms_first else 3
    ones = (row >= 3 - start) & (row < 6 - start)
    rows = jnp.where(ones, 1.0, 0.0)
    for index, part in enumerate(split3(norm)):
        rows = jnp.where(row == start + index, part.astype(F32), rows)
    return rows.astype(BF16)


def source_rows(points, scale):
    parts = split3(points.astype(F32) * scale)
    return jnp.concatenate([*parts, norm_rows(points, scale, True)], 0).T


def target_columns(points, norms):
    return jnp.concatenate([points, points, points, norms], 0)


def tile_of(rows, points, norms):
    product = jnp.dot(rows, target_columns(points, norms), preferred_element_type=F32)
    return jnp.exp2(product).astype(BF16)


def dot_back(values, tile):
    return lax.dot_general(values, tile, (((1,), (1,)), ((), ())), preferred_element_type=F32)


def self_kernel(scale, leaf, points_ref, values_ref, rows_ref, near_ref, norms_ref, tiles_ref):
    norms_ref[...] = norm_rows(points_ref[...], scale, False)
    at = [pl.ds(index * leaf, leaf) for index in range(LPD)]
    for index in range(LPD):
        rows_ref[at[index], :] = source_rows(points_ref[:, at[index]], scale)
    near_ref[...] = jnp.zeros_like(near_ref)

    def add(slot, low, high):
        near_ref[:, at[high]] += jnp.dot(
            values_ref[:, at[low]], tiles_ref[slot], preferred_element_type=F32
        )
        if low != high:
            near_ref[:, at[low]] += dot_back(values_ref[:, at[high]], tiles_ref[slot])

    pairs = [(low, high) for low in range(LPD) for high in range(low, LPD)]
    for slot, (low, high) in enumerate(pairs):
        tiles_ref[slot] = tile_of(
            rows_ref[at[low], :], points_ref[:, at[high]], norms_ref[:, at[high]]
        )
        if slot:
            add(slot - 1, *pairs[slot - 1])
    add(len(pairs) - 1, *pairs[-1])


def pair_kernel(
    scale,
    leaf,
    offset,
    group,
    lower_ref,
    upper_ref,
    rows_ref,
    values_ref,
    other_ref,
    near_in,
    near_ref,
    out_ref,
    norms_ref,
    upper_sum,
    tiles_ref,
):
    dim = other_ref.shape[0] - values_ref.shape[0]
    near_ref[...] = near_in[...]
    upper_sum[...] = jnp.zeros_like(upper_sum)
    norms_ref[...] = norm_rows(other_ref[:dim, :], scale, False)

    def slot_of(index):
        low = lower_ref[0, offset, index]
        start = pl.multiple_of(jnp.maximum(low, 0) * leaf, leaf)
        return low >= 0, start, pl.multiple_of(upper_ref[0, offset, index] * leaf, leaf)

    def add(slot, live, low, high):
        flag = jnp.where(live, 1.0, 0.0).astype(BF16)
        low_at, high_at = pl.ds(low, leaf), pl.ds(high, leaf)
        tile = tiles_ref[slot]
        upper_sum[:, high_at] += jnp.dot(
            values_ref[:, low_at] * flag, tile, preferred_element_type=F32
        )
        near_ref[:, low_at] += dot_back(other_ref[dim:, high_at] * flag, tile)

    @pl.loop(0, lower_ref.shape[2] // group)
    def _(step):
        slots = [slot_of(step * group + index) for index in range(group)]
        some = functools.reduce(jnp.logical_or, [slot[0] for slot in slots])

        @pl.when(some)
        def _():
            for index, (_, low, high) in enumerate(slots):
                tiles_ref[index] = tile_of(
                    rows_ref[pl.ds(low, leaf), :],
                    other_ref[:dim, pl.ds(high, leaf)],
                    norms_ref[:, pl.ds(high, leaf)],
                )
                if index:
                    add(index - 1, *slots[index - 1])
            add(group - 1, *slots[group - 1])

    out_ref[...] = upper_sum[...].astype(BF16)


def picked(index_row, count):
    wide = (count, index_row.shape[1])
    rows = lax.broadcasted_iota(jnp.int32, wide, 0)
    return jnp.where(rows == index_row, 1.0, 0.0).astype(BF16)


def flags_dot(left, right):
    return jnp.dot(left, right, preferred_element_type=F32).astype(BF16)


def rise_kernel(
    levels,
    leaf,
    where_ref,
    points_ref,
    values_ref,
    leaf_pick,
    leaf_assign,
    device_pick,
    device_assign,
    node_pick,
    node_assign,
    share_ref,
    spread_ref,
):
    row_index = where_ref[1]
    picks = picked(device_pick[...], LPD * SKEL)
    assigns = picked(device_assign[...], SKEL)
    for level in range(1, levels + 1):
        heap = (1 << (levels - level)) - 1 + (row_index >> level)
        side = (row_index >> (level - 1)) & 1
        step_pick = node_pick[0, pl.ds(heap, 1), :] - side * SKEL
        picks = flags_dot(picks, picked(step_pick, SKEL))
        both = node_assign[0, pl.ds(heap, 1), :]
        step_assign = jnp.where(side == 0, both[:, :SKEL], both[:, SKEL:])
        assigns = flags_dot(picked(step_assign, SKEL), assigns)
    dim = points_ref.shape[0]
    root_points = jnp.zeros((dim, SKEL), F32)
    root_weights = jnp.zeros((values_ref.shape[0], SKEL), F32)
    for index in range(LPD):
        at = pl.ds(index * leaf, leaf)
        node = slice(index * SKEL, (index + 1) * SKEL)
        chosen = flags_dot(points_ref[:, at], picked(leaf_pick[index : index + 1, :], leaf))
        root_points += jnp.dot(chosen, picks[node], preferred_element_type=F32)
        spread = flags_dot(assigns[:, node], picked(leaf_assign[index : index + 1, :], SKEL))
        spread_ref[:, at] = spread
        root_weights += dot_back(values_ref[:, at], spread)
    share_ref[:dim, :] = root_points
    share_ref[dim:, :] = root_weights


def root_kernel(scale, where_ref, mask_ref, roots_ref, out_ref):
    count, rows, skel = roots_ref.shape
    cols = out_ref.shape[0]
    dim = rows - cols
    target = roots_ref[0, :dim, :].astype(BF16)
    target_norms = norm_rows(target, scale, False)
    total = jnp.zeros((cols, skel), F32)
    for index in range(1, count):
        source = roots_ref[index, :dim, :].astype(BF16)
        flag = mask_ref[0, where_ref[0] ^ index].astype(F32)
        kernel = jnp.exp2(
            jnp.dot(
                source_rows(source, scale),
                target_columns(target, target_norms),
                preferred_element_type=F32,
            )
        )
        weights = roots_ref[index, dim:, :] * flag
        total += jnp.dot(
            weights, kernel, preferred_element_type=F32, precision=lax.Precision.HIGHEST
        )
    out_ref[...] = total


def final_kernel(near_ref, root_ref, spread_ref, *refs):
    back_refs, out_ref = refs[:-1], refs[-1]
    total = near_ref[...]
    for part in split3(root_ref[...]):
        total += jnp.dot(part, spread_ref[...], preferred_element_type=F32)
    for back in back_refs:
        total += back[...].astype(F32)
    out_ref[...] = total


def shape(*dims, dtype=F32):
    return jax.ShapeDtypeStruct(dims, dtype)


def cost(flops, moved, exps=0):
    return pl.CostEstimate(flops=flops, bytes_accessed=moved, transcendentals=exps)


def on_device(
    points,
    vectors,
    leaf_pick,
    leaf_assign,
    device_pick,
    device_assign,
    node_pick,
    node_assign,
    far_mask,
    near_lower,
    near_upper,
):
    dim, device_cols = points.shape
    cols = vectors.shape[0]
    leaf = device_cols // LPD
    scale = 2.0 * KERNEL_RATE / dim * LOG2E
    width = 3 * dim + ROWS_AUG
    gx_count, reach = lax.axis_size("gx"), lax.axis_size("gy")
    levels = reach.bit_length() - 1
    slots = near_lower.shape[2]
    group = next(size for size in (4, 3, 2, 1) if slots % size == 0)
    where = jnp.stack([lax.axis_index("gx"), lax.axis_index("gy")]).astype(jnp.int32)
    tile_flops = 2 * leaf * leaf * (256 + 2 * 256)

    packed = jnp.concatenate([points, vectors], 0)
    others = {o: passed_along(packed, ("gx", "gy"), -o) for o in range(1, reach + 1)}

    share, spread = pl.pallas_call(
        functools.partial(rise_kernel, levels, leaf),
        out_shape=(shape(dim + cols, SKEL), shape(SKEL, device_cols, dtype=BF16)),
        in_specs=[SMEM] + [VMEM] * 8,
        out_specs=(VMEM, VMEM),
        cost_estimate=cost(2**28, 2**20),
        name="rise",
    )(where, points, vectors, leaf_pick, leaf_assign, device_pick, device_assign, node_pick, node_assign)
    for bit in range(levels):
        share = share + swapped(share, "gy", 1 << bit)
    roots = share[None]
    for bit in range(gx_count.bit_length() - 1):
        roots = jnp.concatenate([roots, swapped(roots, "gx", 1 << bit)], 0)

    rows, near = pl.pallas_call(
        functools.partial(self_kernel, scale, leaf),
        out_shape=(shape(device_cols, width, dtype=BF16), shape(cols, device_cols)),
        in_specs=[VMEM, VMEM],
        out_specs=(VMEM, VMEM),
        scratch_shapes=[
            pltpu.VMEM((ROWS_AUG, device_cols), BF16),
            pltpu.VMEM((LPD * (LPD + 1) // 2, leaf, leaf), BF16),
        ],
        cost_estimate=cost(10 * tile_flops, 2**21, 10 * leaf * leaf),
        name="own",
    )(points, vectors)
    backs = []
    for offset in range(reach, 0, -1):
        near, upper = pl.pallas_call(
            functools.partial(pair_kernel, scale, leaf, offset - 1, group),
            out_shape=(shape(cols, device_cols), shape(cols, device_cols, dtype=BF16)),
            in_specs=[SMEM, SMEM] + [VMEM] * 4,
            out_specs=(VMEM, VMEM),
            scratch_shapes=[
                pltpu.VMEM((ROWS_AUG, device_cols), BF16),
                pltpu.VMEM((cols, device_cols), F32),
                pltpu.VMEM((group, leaf, leaf), BF16),
            ],
            cost_estimate=cost(slots * tile_flops, 2**21, slots * leaf * leaf),
            name=f"near{offset}",
        )(near_lower, near_upper, rows, vectors, others[offset], near)
        backs.append(passed_along(upper, ("gx", "gy"), offset))
    root = pl.pallas_call(
        functools.partial(root_kernel, scale),
        out_shape=shape(cols, SKEL),
        in_specs=[SMEM, SMEM, VMEM],
        out_specs=VMEM,
        cost_estimate=cost(2**28, 2**20),
        name="roots",
    )(where, far_mask, roots)
    return pl.pallas_call(
        final_kernel,
        out_shape=shape(cols, device_cols),
        in_specs=[VMEM] * (3 + reach),
        out_specs=VMEM,
        cost_estimate=cost(2**26, 2**20),
        name="sum",
    )(near, root, spread, *backs)


def solution(mesh):
    placed = (
        P(None, ("gx", "gy")),
        P(None, ("gx", "gy")),
        P(("gx", "gy"), None),
        P(("gx", "gy"), None),
        P(("gx", "gy"), None),
        P(("gx", "gy"), None),
        P("gx", None, None),
        P("gx", None, None),
        P("gx", None),
        P(("gx", "gy"), None, None),
        P(("gx", "gy"), None, None),
    )
    return jax.shard_map(
        on_device, mesh=mesh, in_specs=placed, out_specs=P(None, ("gx", "gy")), check_vma=False
    )
```

```python
import functools
import math

import jax
import jax.numpy as jnp
from jax import lax
from jax.experimental import pallas as pl
from jax.experimental.pallas import tpu as pltpu
from jax.sharding import PartitionSpec as P

LPD = 4
SKEL = 128
KERNEL_RATE = 2.0
LOG2E = math.log2(math.e)
ROWS_AUG = 16
F32, BF16 = jnp.float32, jnp.bfloat16
VMEM = pl.BlockSpec(memory_space=pltpu.VMEM)
SMEM = pl.BlockSpec(memory_space=pltpu.SMEM)


def passed_along(value, axis, steps):
    count = lax.axis_size(axis)
    first, last = (max(0, -steps), min(count, count - steps))
    return lax.ppermute(value, axis, [(source, source + steps) for source in range(first, last)])


def swapped(value, axis, mask):
    pairs = [(source, source ^ mask) for source in range(lax.axis_size(axis))]
    return lax.ppermute(value, axis, pairs)


def split3(value):
    first = value.astype(BF16)
    rest = value - first.astype(F32)
    second = rest.astype(BF16)
    third = (rest - second.astype(F32)).astype(BF16)
    return first, second, third


def norm_rows(points, scale, norms_first):
    wide = points.astype(F32)
    norm = -0.5 * scale * jnp.sum(wide * wide, axis=0, keepdims=True)
    row = lax.broadcasted_iota(jnp.int32, (ROWS_AUG, points.shape[1]), 0)
    start = 0 if norms_first else 3
    ones = (row >= 3 - start) & (row < 6 - start)
    rows = jnp.where(ones, 1.0, 0.0)
    for index, part in enumerate(split3(norm)):
        rows = jnp.where(row == start + index, part.astype(F32), rows)
    return rows.astype(BF16)


def source_rows(points, scale):
    parts = split3(points.astype(F32) * scale)
    return jnp.concatenate([*parts, norm_rows(points, scale, True)], 0).T


def target_columns(points, norms):
    return jnp.concatenate([points, points, points, norms], 0)


def tile_of(rows, points, norms):
    product = jnp.dot(rows, target_columns(points, norms), preferred_element_type=F32)
    return jnp.exp2(product).astype(BF16)


def dot_back(values, tile):
    return lax.dot_general(values, tile, (((1,), (1,)), ((), ())), preferred_element_type=F32)


def self_kernel(scale, leaf, points_ref, values_ref, rows_ref, near_ref, norms_ref, tiles_ref):
    norms_ref[...] = norm_rows(points_ref[...], scale, False)
    at = [pl.ds(index * leaf, leaf) for index in range(LPD)]
    for index in range(LPD):
        rows_ref[at[index], :] = source_rows(points_ref[:, at[index]], scale)
    near_ref[...] = jnp.zeros_like(near_ref)

    def add(slot, low, high):
        near_ref[:, at[high]] += jnp.dot(
            values_ref[:, at[low]], tiles_ref[slot], preferred_element_type=F32
        )
        if low != high:
            near_ref[:, at[low]] += dot_back(values_ref[:, at[high]], tiles_ref[slot])

    pairs = [(low, high) for low in range(LPD) for high in range(low, LPD)]
    for slot, (low, high) in enumerate(pairs):
        tiles_ref[slot] = tile_of(
            rows_ref[at[low], :], points_ref[:, at[high]], norms_ref[:, at[high]]
        )
        if slot:
            add(slot - 1, *pairs[slot - 1])
    add(len(pairs) - 1, *pairs[-1])


def pair_kernel(
    scale,
    leaf,
    reach,
    partner,
    group,
    where_ref,
    lower_ref,
    upper_ref,
    rows_ref,
    values_ref,
    other_ref,
    near_in,
    near_ref,
    out_ref,
    norms_ref,
    upper_sum,
    tiles_ref,
):
    dim = other_ref.shape[0] - values_ref.shape[0]
    row_index = where_ref[1]
    offset = lax.rem((row_index ^ partner) - row_index + reach - 1, reach)
    upper_sum[...] = jnp.zeros_like(upper_sum)
    norms_ref[...] = norm_rows(other_ref[:dim, :], scale, False)

    def slot_of(index):
        low = lower_ref[0, offset, index]
        start = pl.multiple_of(jnp.maximum(low, 0) * leaf, leaf)
        return low >= 0, start, pl.multiple_of(upper_ref[0, offset, index] * leaf, leaf)

    def add(slot, live, low, high):
        flag = jnp.where(live, 1.0, 0.0).astype(BF16)
        low_at, high_at = pl.ds(low, leaf), pl.ds(high, leaf)
        tile = tiles_ref[slot]
        upper_sum[:, high_at] += jnp.dot(
            values_ref[:, low_at] * flag, tile, preferred_element_type=F32
        )
        near_ref[:, low_at] += dot_back(other_ref[dim:, high_at] * flag, tile)

    @pl.loop(0, lower_ref.shape[2] // group)
    def _(step):
        slots = [slot_of(step * group + index) for index in range(group)]
        some = functools.reduce(jnp.logical_or, [slot[0] for slot in slots])

        @pl.when(some)
        def _():
            for index, (_, low, high) in enumerate(slots):
                tiles_ref[index] = tile_of(
                    rows_ref[pl.ds(low, leaf), :],
                    other_ref[:dim, pl.ds(high, leaf)],
                    norms_ref[:, pl.ds(high, leaf)],
                )
                if index:
                    add(index - 1, *slots[index - 1])
            add(group - 1, *slots[group - 1])

    out_ref[...] = upper_sum[...].astype(BF16)


def picked(index_row, count):
    wide = (count, index_row.shape[1])
    rows = lax.broadcasted_iota(jnp.int32, wide, 0)
    return jnp.where(rows == index_row, 1.0, 0.0).astype(BF16)


def flags_dot(left, right):
    return jnp.dot(left, right, preferred_element_type=F32).astype(BF16)


def rise_kernel(
    levels,
    leaf,
    points_ref,
    values_ref,
    leaf_pick,
    leaf_assign,
    device_pick,
    device_assign,
    tables_ref,
    share_ref,
    spread_ref,
):
    picks = picked(device_pick[...], LPD * SKEL)
    assigns = picked(device_assign[...], SKEL)
    for level in range(levels):
        step_pick = tables_ref[2 * level : 2 * level + 1, :]
        step_assign = tables_ref[2 * level + 1 : 2 * level + 2, :]
        picks = flags_dot(picks, picked(step_pick, SKEL))
        assigns = flags_dot(picked(step_assign, SKEL), assigns)
    dim = points_ref.shape[0]
    root_points = jnp.zeros((dim, SKEL), F32)
    root_weights = jnp.zeros((values_ref.shape[0], SKEL), F32)
    for index in range(LPD):
        at = pl.ds(index * leaf, leaf)
        node = slice(index * SKEL, (index + 1) * SKEL)
        chosen = flags_dot(points_ref[:, at], picked(leaf_pick[index : index + 1, :], leaf))
        root_points += jnp.dot(chosen, picks[node], preferred_element_type=F32)
        spread = flags_dot(assigns[:, node], picked(leaf_assign[index : index + 1, :], SKEL))
        spread_ref[:, at] = spread
        root_weights += dot_back(values_ref[:, at], spread)
    share_ref[:dim, :] = root_points
    share_ref[dim:, :] = root_weights


def root_kernel(scale, where_ref, mask_ref, roots_ref, out_ref):
    count, cols = roots_ref.shape[0], out_ref.shape[0]
    dim = roots_ref.shape[1] - cols
    target = source_rows(roots_ref[0, :dim, :].astype(BF16), scale)
    flags = [mask_ref[0, where_ref[0] ^ index].astype(F32) for index in range(1, count)]
    weights = [roots_ref[index, dim:, :] * flag for index, flag in enumerate(flags, 1)]
    sources = [roots_ref[index, :dim, :].astype(BF16) for index in range(1, count)]
    source = jnp.concatenate(sources, 1)
    product = jnp.dot(
        target,
        target_columns(source, norm_rows(source, scale, False)),
        preferred_element_type=F32,
    )
    out_ref[...] = lax.dot_general(
        jnp.concatenate(weights, 1),
        jnp.exp2(product),
        (((1,), (1,)), ((), ())),
        preferred_element_type=F32,
        precision=lax.Precision.HIGHEST,
    )


def fall_kernel(near_ref, root_ref, spread_ref, out_ref):
    total = near_ref[...]
    for part in split3(root_ref[...]):
        total += jnp.dot(part, spread_ref[...], preferred_element_type=F32)
    out_ref[...] = total


def shape(*dims, dtype=F32):
    return jax.ShapeDtypeStruct(dims, dtype)


def kept(*dims, dtype=F32):
    return pltpu.VMEM(dims, dtype)


def held(value):
    return pltpu.with_memory_space_constraint(value, pltpu.VMEM)


def cost(flops, moved, exps=0):
    return pl.CostEstimate(flops=flops, bytes_accessed=moved, transcendentals=exps)


def on_device(
    points,
    vectors,
    leaf_pick,
    leaf_assign,
    device_pick,
    device_assign,
    node_pick,
    node_assign,
    far_mask,
    near_lower,
    near_upper,
):
    dim, device_cols = points.shape
    cols = vectors.shape[0]
    leaf = device_cols // LPD
    scale = 2.0 * KERNEL_RATE / dim * LOG2E
    width = 3 * dim + ROWS_AUG
    gx_count, reach = lax.axis_size("gx"), lax.axis_size("gy")
    levels = reach.bit_length() - 1
    slots = near_lower.shape[2]
    group = next(size for size in (4, 3, 2, 1) if slots % size == 0)
    row_index = lax.axis_index("gy")
    where = jnp.stack([lax.axis_index("gx"), row_index]).astype(jnp.int32)
    tile_flops = 2 * leaf * leaf * (256 + 2 * 256)

    def side_of(level):
        return (row_index >> (level - 1)) & 1

    packed = jnp.concatenate([points, vectors], 0)
    ahead = passed_along(packed, "gx", -1)

    tables = []
    for level in range(1, levels + 1):
        heap = (reach >> level) - 1 + (row_index >> level)
        tables.append(lax.dynamic_slice(node_pick[0], (heap, 0), (1, SKEL)) - side_of(level) * SKEL)
        tables.append(
            lax.dynamic_slice(node_assign[0], (heap, side_of(level) * SKEL), (1, SKEL))
        )
    share, spread = pl.pallas_call(
        functools.partial(rise_kernel, levels, leaf),
        out_shape=(shape(dim + cols, SKEL), kept(SKEL, device_cols, dtype=BF16)),
        in_specs=[VMEM] * 7,
        out_specs=(VMEM, VMEM),
        cost_estimate=cost(2**28, 2**20),
        name="rise",
    )(points, vectors, leaf_pick, leaf_assign, device_pick, device_assign, jnp.concatenate(tables, 0))
    for bit in range(levels):
        share = share + swapped(share, "gy", 1 << bit)
    roots = share[None]
    for bit in range(gx_count.bit_length() - 1):
        roots = jnp.concatenate([roots, swapped(roots, "gx", 1 << bit)], 0)

    rows, near = pl.pallas_call(
        functools.partial(self_kernel, scale, leaf),
        out_shape=(kept(device_cols, width, dtype=BF16), kept(cols, device_cols)),
        in_specs=[VMEM, VMEM],
        out_specs=(VMEM, VMEM),
        scratch_shapes=[
            pltpu.VMEM((ROWS_AUG, device_cols), BF16),
            pltpu.VMEM((LPD * (LPD + 1) // 2, leaf, leaf), BF16),
        ],
        cost_estimate=cost(10 * tile_flops, 2**21, 10 * leaf * leaf),
        name="own",
    )(points, vectors)

    def meet(partner, other, near):
        return pl.pallas_call(
            functools.partial(pair_kernel, scale, leaf, reach, partner, group),
            out_shape=(kept(cols, device_cols), shape(cols, device_cols, dtype=BF16)),
            in_specs=[SMEM] * 3 + [VMEM] * 4,
            out_specs=(VMEM, VMEM),
            scratch_shapes=[
                pltpu.VMEM((ROWS_AUG, device_cols), BF16),
                pltpu.VMEM((cols, device_cols), F32),
                pltpu.VMEM((group, leaf, leaf), BF16),
            ],
            input_output_aliases={6: 0},
            cost_estimate=cost(slots * tile_flops, 2**21, slots * leaf * leaf),
            name=f"near{partner}",
        )(where, near_lower, near_upper, held(rows), vectors, held(other), held(near))

    others = {}
    for bit in range(levels):
        payload = jnp.where(side_of(bit + 1) == 1, packed, ahead)
        for partner in range(1 << bit, 2 << bit):
            others[partner] = swapped(payload, "gy", partner)
    mine, onward = [], []
    for partner in range(1, reach):
        near, upper = meet(partner, others[partner], near)
        back = swapped(upper, "gy", partner).astype(F32)
        upper_side = side_of(partner.bit_length()) == 1
        mine.append(jnp.where(upper_side, back, 0.0))
        onward.append(jnp.where(upper_side, 0.0, back))
    near, upper = meet(0, ahead, near)
    forward = functools.reduce(jnp.add, onward, upper.astype(F32)).astype(BF16)
    landed = passed_along(forward, "gx", 1)
    root = pl.pallas_call(
        functools.partial(root_kernel, scale),
        out_shape=shape(cols, SKEL),
        in_specs=[SMEM, SMEM, VMEM],
        out_specs=VMEM,
        cost_estimate=cost(2**28, 2**20),
        name="roots",
    )(where, far_mask, roots)
    local = pl.pallas_call(
        fall_kernel,
        out_shape=shape(cols, device_cols),
        in_specs=[VMEM] * 3,
        out_specs=VMEM,
        cost_estimate=cost(2**26, 2**20),
        name="fall",
    )(held(near), root, held(spread))
    return functools.reduce(jnp.add, mine, local) + landed.astype(F32)


def solution(mesh):
    placed = (
        P(None, ("gx", "gy")),
        P(None, ("gx", "gy")),
        P(("gx", "gy"), None),
        P(("gx", "gy"), None),
        P(("gx", "gy"), None),
        P(("gx", "gy"), None),
        P("gx", None, None),
        P("gx", None, None),
        P("gx", None),
        P(("gx", "gy"), None, None),
        P(("gx", "gy"), None, None),
    )
    return jax.shard_map(
        on_device, mesh=mesh, in_specs=placed, out_specs=P(None, ("gx", "gy")), check_vma=False
    )
```

```python
import functools
import math

import jax
import jax.numpy as jnp
from jax import lax
from jax.experimental import pallas as pl
from jax.experimental.pallas import tpu as pltpu
from jax.sharding import PartitionSpec as P


LPD = 4
SKEL = 128
KERNEL_RATE = 2.0
LOG2E = math.log2(math.e)
ROWS_AUG = 16
F32, BF16 = jnp.float32, jnp.bfloat16
VMEM = pl.BlockSpec(memory_space=pltpu.VMEM)


def passed_along(value, axis, steps):
    count = lax.axis_size(axis)
    first, last = (max(0, -steps), min(count, count - steps))
    pairs = [(source, source + steps) for source in range(first, last)]
    return lax.ppermute(value, axis, pairs)


def swapped(value, axis, mask):
    pairs = [(source, source ^ mask) for source in range(lax.axis_size(axis))]
    return lax.ppermute(value, axis, pairs)


def split3(value):
    first = value.astype(BF16)
    rest = value - first.astype(F32)
    second = rest.astype(BF16)
    third = (rest - second.astype(F32)).astype(BF16)
    return first, second, third


def norm_rows(points, scale, norms_first):
    wide = points.astype(F32)
    norm = -0.5 * scale * jnp.sum(wide * wide, axis=0, keepdims=True)
    row = lax.broadcasted_iota(jnp.int32, (ROWS_AUG, points.shape[1]), 0)
    start = 0 if norms_first else 3
    ones = (row >= 3 - start) & (row < 6 - start)
    rows = jnp.where(ones, 1.0, 0.0)
    for index, part in enumerate(split3(norm)):
        rows = jnp.where(row == start + index, part.astype(F32), rows)
    return rows.astype(BF16)


def source_rows(points, scale):
    parts = split3(points.astype(F32) * scale)
    return jnp.concatenate([*parts, norm_rows(points, scale, True)], 0).T


def target_columns(points, norms):
    return jnp.concatenate([points, points, points, norms], 0)


def tile_of(rows, points, norms):
    product = jnp.dot(rows, target_columns(points, norms), preferred_element_type=F32)
    return jnp.exp2(product).astype(BF16)


def dot_back(values, tile):
    return lax.dot_general(values, tile, (((1,), (1,)), ((), ())), preferred_element_type=F32)


def self_kernel(scale, leaf, own_ref, rows_ref, near_ref, norms_ref, tiles_ref):
    dim = own_ref.shape[0] - near_ref.shape[0]
    points_ref, values_ref = own_ref.at[:dim, :], own_ref.at[dim:, :]
    norms_ref[...] = norm_rows(points_ref[...], scale, False)
    at = [pl.ds(index * leaf, leaf) for index in range(LPD)]
    for index in range(LPD):
        rows_ref[at[index], :] = source_rows(points_ref[:, at[index]], scale)
    near_ref[...] = jnp.zeros_like(near_ref)

    def add(slot, low, high):
        near_ref[:, at[high]] += jnp.dot(
            values_ref[:, at[low]], tiles_ref[slot], preferred_element_type=F32
        )
        if low != high:
            near_ref[:, at[low]] += dot_back(values_ref[:, at[high]], tiles_ref[slot])

    pairs = [(low, high) for low in range(LPD) for high in range(low, LPD)]
    for slot, (low, high) in enumerate(pairs):
        tiles_ref[slot] = tile_of(
            rows_ref[at[low], :], points_ref[:, at[high]], norms_ref[:, at[high]]
        )
        if slot:
            add(slot - 1, *pairs[slot - 1])
    add(len(pairs) - 1, *pairs[-1])


def pair_kernel(
    scale,
    leaf,
    partner,
    group,
    lower_ref,
    upper_ref,
    rows_ref,
    own_ref,
    other_ref,
    near_in,
    near_ref,
    out_ref,
    norms_ref,
    upper_sum,
    tiles_ref,
):
    cols = near_ref.shape[0]
    dim = own_ref.shape[0] - cols
    reach, row_index = lax.axis_size("gy"), lax.axis_index("gy")
    offset = lax.rem((row_index ^ partner) - row_index + reach - 1, reach)
    lower, upper = (ref[0, pl.ds(offset, 1), :] for ref in (lower_ref, upper_ref))
    codes = jnp.where(lower >= 0, lower * LPD + upper, -1)
    upper_sum[...] = jnp.zeros_like(upper_sum)
    norms_ref[...] = norm_rows(other_ref[:dim, :], scale, False)

    def slot_of(index):
        code = codes[0, index]
        pair = jnp.maximum(code, 0)
        low = pl.multiple_of(lax.div(pair, LPD) * leaf, leaf)
        return code >= 0, low, pl.multiple_of(lax.rem(pair, LPD) * leaf, leaf)

    def add(slot, live, low, high):
        flag = jnp.where(live, 1.0, 0.0).astype(BF16)
        low_at, high_at = pl.ds(low, leaf), pl.ds(high, leaf)
        tile = tiles_ref[slot]
        upper_sum[:, high_at] += jnp.dot(
            own_ref[dim:, low_at] * flag, tile, preferred_element_type=F32
        )
        near_ref[:, low_at] += dot_back(other_ref[dim:, high_at] * flag, tile)

    def some_slots(slots):
        for index, (_, low, high) in enumerate(slots):
            tiles_ref[index] = tile_of(
                rows_ref[pl.ds(low, leaf), :],
                other_ref[:dim, pl.ds(high, leaf)],
                norms_ref[:, pl.ds(high, leaf)],
            )
            if index:
                add(index - 1, *slots[index - 1])
        add(group - 1, *slots[group - 1])

    for start in range(0, lower_ref.shape[2], group):
        slots = [slot_of(index) for index in range(start, start + group)]
        live = functools.reduce(jnp.logical_or, [slot[0] for slot in slots])
        pl.when(live)(functools.partial(some_slots, slots))
    out_ref[...] = upper_sum[...].astype(BF16)


def picked(index_row, count):
    wide = (count, index_row.shape[1])
    rows = lax.broadcasted_iota(jnp.int32, wide, 0)
    return jnp.where(rows == index_row, 1.0, 0.0).astype(BF16)


def flags_dot(left, right):
    return jnp.dot(left, right, preferred_element_type=F32).astype(BF16)


def rise_kernel(
    levels,
    leaf,
    dim,
    own_ref,
    leaf_pick,
    leaf_assign,
    device_pick,
    device_assign,
    node_pick,
    node_assign,
    share_ref,
    spread_ref,
):
    row_index = lax.axis_index("gy")
    picks = picked(device_pick[...], LPD * SKEL)
    assigns = picked(device_assign[...], SKEL)
    for level in range(1, levels + 1):
        heap = (1 << (levels - level)) - 1 + (row_index >> level)
        side = (row_index >> (level - 1)) & 1
        both = node_assign[heap]
        step_assign = jnp.where(side == 0, both[:, :SKEL], both[:, SKEL:])
        picks = flags_dot(picks, picked(node_pick[heap] - side * SKEL, SKEL))
        assigns = flags_dot(picked(step_assign, SKEL), assigns)
    root_points = jnp.zeros((dim, SKEL), F32)
    root_weights = jnp.zeros((own_ref.shape[0] - dim, SKEL), F32)
    for index in range(LPD):
        at = pl.ds(index * leaf, leaf)
        node = slice(index * SKEL, (index + 1) * SKEL)
        chosen = flags_dot(own_ref[:dim, at], picked(leaf_pick[index : index + 1, :], leaf))
        root_points += jnp.dot(chosen, picks[node], preferred_element_type=F32)
        spread = flags_dot(assigns[:, node], picked(leaf_assign[index : index + 1, :], SKEL))
        spread_ref[:, at] = spread
        root_weights += dot_back(own_ref[dim:, at], spread)
    share_ref[:dim, :] = root_points
    share_ref[dim:, :] = root_weights


def root_kernel(scale, mask_ref, *refs):
    parts, out_ref = refs[:-1], refs[-1]
    roots = [part[index] for part in parts for index in range(part.shape[0])]
    dim = roots[0].shape[0] - out_ref.shape[0]
    target = source_rows(roots[0][:dim].astype(BF16), scale)
    group = lax.broadcasted_iota(jnp.int32, mask_ref.shape, 1) ^ lax.axis_index("gx")
    weights = []
    for index in range(1, len(roots)):
        flag = jnp.sum(jnp.where(group == index, mask_ref[...], 0), axis=1, keepdims=True)
        weights.append(roots[index][dim:] * flag.astype(F32))
    source = jnp.concatenate([root[:dim].astype(BF16) for root in roots[1:]], 1)
    product = jnp.dot(
        target,
        target_columns(source, norm_rows(source, scale, False)),
        preferred_element_type=F32,
    )
    out_ref[...] = lax.dot_general(
        jnp.concatenate(weights, 1),
        jnp.exp2(product),
        (((1,), (1,)), ((), ())),
        preferred_element_type=F32,
        precision=lax.Precision.HIGHEST,
    )


def route_kernel(own_ref, ahead_ref, *out_refs):
    row_index = lax.axis_index("gy")
    for bit, out_ref in enumerate(out_refs):
        upper_side = (row_index >> bit) & 1 == 1

        @pl.when(upper_side)
        def _():
            out_ref[...] = own_ref[...]

        @pl.when(jnp.logical_not(upper_side))
        def _():
            out_ref[...] = ahead_ref[...]


def add_kernel(left_ref, right_ref, out_ref):
    out_ref[...] = (left_ref[...] + right_ref[...]).reshape(out_ref.shape)


def join_kernel(*refs):
    parts, out_ref = refs[:-1], refs[-1]
    start = 0
    for part in parts:
        out_ref[pl.ds(start, part.shape[0])] = part[...]
        start += part.shape[0]


def onward_kernel(partners, *refs):
    row_index = lax.axis_index("gy")
    total = refs[0][...].astype(F32)
    for partner, ref in zip(partners, refs[1:-1]):
        lower_side = (row_index >> (partner.bit_length() - 1)) & 1 == 0
        total += ref[...].astype(F32) * jnp.where(lower_side, 1.0, 0.0)
    refs[-1][...] = total.astype(BF16)


def fall_kernel(partners, near_ref, root_ref, spread_ref, *refs):
    row_index = lax.axis_index("gy")
    total = near_ref[...]
    for part in split3(root_ref[...]):
        total += jnp.dot(part, spread_ref[...], preferred_element_type=F32)
    for partner, ref in zip(partners, refs[:-1]):
        upper_side = (row_index >> (partner.bit_length() - 1)) & 1 == 1
        total += ref[...].astype(F32) * jnp.where(upper_side, 1.0, 0.0)
    refs[-1][...] = total


def last_kernel(local_ref, *refs):
    total = local_ref[...]
    for ref in refs[:-1]:
        total += ref[...].astype(F32)
    refs[-1][...] = total


def shape(*dims, dtype=F32):
    return jax.ShapeDtypeStruct(dims, dtype)


def kept(*dims, dtype=F32):
    return pltpu.VMEM(dims, dtype)


def run(kernel, outs, *args, flops=2**20, memory=4, scratch=(), aliases=None):
    many = isinstance(outs, tuple)
    return pl.pallas_call(
        kernel,
        out_shape=outs,
        in_specs=[VMEM] * len(args),
        out_specs=(VMEM,) * len(outs) if many else VMEM,
        scratch_shapes=list(scratch),
        input_output_aliases=aliases or {},
        cost_estimate=pl.CostEstimate(flops=flops, bytes_accessed=2**16, transcendentals=0),
        compiler_params=pltpu.CompilerParams(vmem_limit_bytes=memory * 2**20),
    )(*[pltpu.with_memory_space_constraint(arg, pltpu.VMEM) for arg in args])


def landing(partner, back):
    reach, count = lax.axis_size("gy"), lax.axis_size("gx") * lax.axis_size("gy")
    pairs = []
    for source in range(count):
        row = source % reach
        step = ((row ^ partner) - row - 1) % reach + 1
        if source + step < count:
            pairs.append((source, source + step))
    return lax.ppermute(back, ("gx", "gy"), pairs)


def on_device(
    points,
    vectors,
    leaf_pick,
    leaf_assign,
    device_pick,
    device_assign,
    node_pick,
    node_assign,
    far_mask,
    near_lower,
    near_upper,
):
    dim, device_cols = points.shape
    cols = vectors.shape[0]
    leaf = device_cols // LPD
    scale = 2.0 * KERNEL_RATE / dim * LOG2E
    width = 3 * dim + ROWS_AUG
    gx_count, reach = lax.axis_size("gx"), lax.axis_size("gy")
    levels = reach.bit_length() - 1
    slots = near_lower.shape[2]
    group = next(size for size in (4, 3, 2, 1) if slots % size == 0)
    tile_flops = 2 * leaf * leaf * (256 + 2 * 256)
    block = kept(dim + cols, device_cols, dtype=BF16)
    root_shape = (dim + cols, SKEL)

    packed = jnp.concatenate([points, vectors], 0)
    ahead = passed_along(packed, "gx", -1)

    share, spread = run(
        functools.partial(rise_kernel, levels, leaf, dim),
        (kept(*root_shape), kept(SKEL, device_cols, dtype=BF16)),
        packed,
        leaf_pick,
        leaf_assign,
        device_pick,
        device_assign,
        jnp.transpose(node_pick, (1, 0, 2)),
        jnp.transpose(node_assign, (1, 0, 2)),
        flops=2**29,
        memory=6,
    )
    for bit in range(levels):
        outs = kept(*root_shape) if bit + 1 < levels else kept(1, *root_shape)
        share = run(add_kernel, outs, share, swapped(share, "gy", 1 << bit))
    roots, sent = [share], share
    for bit in range(gx_count.bit_length() - 1):
        if bit:
            sent = run(join_kernel, kept(1 << bit, *root_shape), *roots)
        roots.append(swapped(sent, "gx", 1 << bit))

    rows, near = run(
        functools.partial(self_kernel, scale, leaf),
        (kept(device_cols, width, dtype=BF16), kept(cols, device_cols)),
        packed,
        flops=10 * tile_flops,
        memory=12,
        scratch=[
            pltpu.VMEM((ROWS_AUG, device_cols), BF16),
            pltpu.VMEM((LPD * (LPD + 1) // 2, leaf, leaf), BF16),
        ],
    )

    def meet(partner, other, near):
        return run(
            functools.partial(pair_kernel, scale, leaf, partner, group),
            (kept(cols, device_cols), kept(cols, device_cols, dtype=BF16)),
            near_lower,
            near_upper,
            rows,
            packed,
            other,
            near,
            flops=slots * tile_flops,
            memory=10,
            scratch=[
                pltpu.VMEM((ROWS_AUG, device_cols), BF16),
                pltpu.VMEM((cols, device_cols), F32),
                pltpu.VMEM((group, leaf, leaf), BF16),
            ],
            aliases={5: 0},
        )

    payloads = run(route_kernel, (block,) * levels, packed, ahead)
    others = [ahead]
    for partner in range(1, reach):
        others.append(swapped(payloads[partner.bit_length() - 1], "gy", partner))
    near, first_upper = meet(0, ahead, near)
    partners, backs = list(range(1, reach - 1)), []
    for partner in partners:
        near, upper = meet(partner, others[partner], near)
        backs.append(swapped(upper, "gy", partner))
    near, upper = meet(reach - 1, others[reach - 1], near)
    direct = landing(reach - 1, upper)
    onward = run(
        functools.partial(onward_kernel, partners),
        kept(cols, device_cols, dtype=BF16),
        first_upper,
        *backs,
    )
    landed = passed_along(onward, "gx", 1)
    root = run(
        functools.partial(root_kernel, scale), kept(cols, SKEL), far_mask, *roots, flops=2**28
    )
    local = run(
        functools.partial(fall_kernel, partners),
        kept(cols, device_cols),
        near,
        root,
        spread,
        *backs,
        flops=2**26,
    )
    return run(last_kernel, shape(cols, device_cols), local, landed, direct)


def solution(mesh):
    placed = (
        P(None, ("gx", "gy")),
        P(None, ("gx", "gy")),
        P(("gx", "gy"), None),
        P(("gx", "gy"), None),
        P(("gx", "gy"), None),
        P(("gx", "gy"), None),
        P("gx", None, None),
        P("gx", None, None),
        P("gx", None),
        P(("gx", "gy"), None, None),
        P(("gx", "gy"), None, None),
    )


    return jax.shard_map(
        on_device, mesh=mesh, in_specs=placed, out_specs=P(None, ("gx", "gy")), check_vma=False
    )
```

```python
import functools
import math

import jax
import jax.numpy as jnp
from jax import lax
from jax.experimental import pallas as pl
from jax.experimental.pallas import tpu as pltpu
from jax.sharding import PartitionSpec as P


LPD = 4
SKEL = 128
KERNEL_RATE = 2.0
LOG2E = math.log2(math.e)
ROWS_AUG = 16
F32, BF16 = jnp.float32, jnp.bfloat16
VMEM = pl.BlockSpec(memory_space=pltpu.VMEM)


def passed_along(value, axis, steps):
    count = lax.axis_size(axis)
    first, last = (max(0, -steps), min(count, count - steps))
    pairs = [(source, source + steps) for source in range(first, last)]
    return lax.ppermute(value, axis, pairs)


def swapped(value, axis, mask):
    pairs = [(source, source ^ mask) for source in range(lax.axis_size(axis))]
    return lax.ppermute(value, axis, pairs)


def split3(value):
    first = value.astype(BF16)
    rest = value - first.astype(F32)
    second = rest.astype(BF16)
    third = (rest - second.astype(F32)).astype(BF16)
    return first, second, third


def norm_rows(points, scale, norms_first):
    wide = points.astype(F32)
    norm = -0.5 * scale * jnp.sum(wide * wide, axis=0, keepdims=True)
    row = lax.broadcasted_iota(jnp.int32, (ROWS_AUG, points.shape[1]), 0)
    start = 0 if norms_first else 3
    ones = (row >= 3 - start) & (row < 6 - start)
    rows = jnp.where(ones, 1.0, 0.0)
    for index, part in enumerate(split3(norm)):
        rows = jnp.where(row == start + index, part.astype(F32), rows)
    return rows.astype(BF16)


def source_rows(points, scale):
    parts = split3(points.astype(F32) * scale)
    return jnp.concatenate([*parts, norm_rows(points, scale, True)], 0).T


def target_columns(points, norms):
    return jnp.concatenate([points, points, points, norms], 0)


def tile_of(rows, points, norms):
    product = jnp.dot(rows, target_columns(points, norms), preferred_element_type=F32)
    return jnp.exp2(product).astype(BF16)


def dot_back(values, tile):
    return lax.dot_general(values, tile, (((1,), (1,)), ((), ())), preferred_element_type=F32)


def self_kernel(scale, leaf, own_ref, rows_ref, near_ref, norms_ref, tiles_ref, turned_ref):
    dim = own_ref.shape[0] - near_ref.shape[0]
    points_ref, values_ref = own_ref.at[:dim, :], own_ref.at[dim:, :]
    norms_ref[...] = norm_rows(points_ref[...], scale, False)
    at = [pl.ds(index * leaf, leaf) for index in range(LPD)]
    for index in range(LPD):
        rows_ref[at[index], :] = source_rows(points_ref[:, at[index]], scale)
    near_ref[...] = jnp.zeros_like(near_ref)

    def add(slot, low, high):
        near_ref[:, at[high]] += jnp.dot(
            values_ref[:, at[low]], tiles_ref[slot], preferred_element_type=F32
        )
        if low != high:
            near_ref[:, at[low]] += jnp.dot(
                values_ref[:, at[high]], turned_ref[slot], preferred_element_type=F32
            )

    pairs = [(low, high) for low in range(LPD) for high in range(low, LPD)]
    for slot, (low, high) in enumerate(pairs):
        tile = tile_of(rows_ref[at[low], :], points_ref[:, at[high]], norms_ref[:, at[high]])
        tiles_ref[slot] = tile
        if low != high:
            turned_ref[slot] = tile.T
        if slot:
            add(slot - 1, *pairs[slot - 1])
    add(len(pairs) - 1, *pairs[-1])


def pair_kernel(
    scale,
    leaf,
    partner,
    group,
    lower_ref,
    upper_ref,
    rows_ref,
    own_ref,
    other_ref,
    near_in,
    near_ref,
    out_ref,
    norms_ref,
    upper_sum,
    tiles_ref,
    turned_ref,
):
    cols = near_ref.shape[0]
    dim = own_ref.shape[0] - cols
    reach, row_index = lax.axis_size("gy"), lax.axis_index("gy")
    offset = lax.rem((row_index ^ partner) - row_index + reach - 1, reach)
    lower, upper = (ref[0, pl.ds(offset, 1), :] for ref in (lower_ref, upper_ref))
    codes = jnp.where(lower >= 0, lower * LPD + upper, -1)
    upper_sum[...] = jnp.zeros_like(upper_sum)
    norms_ref[...] = norm_rows(other_ref[:dim, :], scale, False)

    def slot_of(index):
        code = codes[0, index]
        pair = jnp.maximum(code, 0)
        low = pl.multiple_of(lax.div(pair, LPD) * leaf, leaf)
        return code >= 0, low, pl.multiple_of(lax.rem(pair, LPD) * leaf, leaf)

    def add(slot, live, low, high):
        flag = jnp.where(live, 1.0, 0.0).astype(BF16)
        low_at, high_at = pl.ds(low, leaf), pl.ds(high, leaf)
        upper_sum[:, high_at] += jnp.dot(
            own_ref[dim:, low_at] * flag, tiles_ref[slot], preferred_element_type=F32
        )
        near_ref[:, low_at] += jnp.dot(
            other_ref[dim:, high_at] * flag, turned_ref[slot], preferred_element_type=F32
        )

    def some_slots(slots):
        for index, (_, low, high) in enumerate(slots):
            tile = tile_of(
                rows_ref[pl.ds(low, leaf), :],
                other_ref[:dim, pl.ds(high, leaf)],
                norms_ref[:, pl.ds(high, leaf)],
            )
            tiles_ref[index] = tile
            turned_ref[index] = tile.T
            if index:
                add(index - 1, *slots[index - 1])
        add(group - 1, *slots[group - 1])

    for start in range(0, lower_ref.shape[2], group):
        slots = [slot_of(index) for index in range(start, start + group)]
        live = functools.reduce(jnp.logical_or, [slot[0] for slot in slots])
        pl.when(live)(functools.partial(some_slots, slots))
    out_ref[...] = upper_sum[...].astype(BF16)


def picked(index_row, count):
    wide = (count, index_row.shape[1])
    rows = lax.broadcasted_iota(jnp.int32, wide, 0)
    return jnp.where(rows == index_row, 1.0, 0.0).astype(BF16)


def flags_dot(left, right):
    return jnp.dot(left, right, preferred_element_type=F32).astype(BF16)


def rise_kernel(
    levels,
    leaf,
    dim,
    own_ref,
    leaf_pick,
    leaf_assign,
    device_pick,
    device_assign,
    node_pick,
    node_assign,
    share_ref,
    spread_ref,
):
    row_index = lax.axis_index("gy")
    picks = picked(device_pick[...], LPD * SKEL)
    assigns = picked(device_assign[...], SKEL)
    for level in range(1, levels + 1):
        heap = (1 << (levels - level)) - 1 + (row_index >> level)
        side = (row_index >> (level - 1)) & 1
        both = node_assign[heap]
        step_assign = jnp.where(side == 0, both[:, :SKEL], both[:, SKEL:])
        picks = flags_dot(picks, picked(node_pick[heap] - side * SKEL, SKEL))
        assigns = flags_dot(picked(step_assign, SKEL), assigns)
    root_points = jnp.zeros((dim, SKEL), F32)
    root_weights = jnp.zeros((own_ref.shape[0] - dim, SKEL), F32)
    for index in range(LPD):
        at = pl.ds(index * leaf, leaf)
        node = slice(index * SKEL, (index + 1) * SKEL)
        chosen = flags_dot(own_ref[:dim, at], picked(leaf_pick[index : index + 1, :], leaf))
        root_points += jnp.dot(chosen, picks[node], preferred_element_type=F32)
        spread = flags_dot(assigns[:, node], picked(leaf_assign[index : index + 1, :], SKEL))
        spread_ref[:, at] = spread
        root_weights += dot_back(own_ref[dim:, at], spread)
    share_ref[:dim, :] = root_points
    share_ref[dim:, :] = root_weights


def root_kernel(scale, mask_ref, *refs):
    parts, out_ref = refs[:-1], refs[-1]
    roots = [part[index] for part in parts for index in range(part.shape[0])]
    dim = roots[0].shape[0] - out_ref.shape[0]
    target = source_rows(roots[0][:dim].astype(BF16), scale)
    group = lax.broadcasted_iota(jnp.int32, mask_ref.shape, 1) ^ lax.axis_index("gx")
    weights = []
    for index in range(1, len(roots)):
        flag = jnp.sum(jnp.where(group == index, mask_ref[...], 0), axis=1, keepdims=True)
        weights.append(roots[index][dim:] * flag.astype(F32))
    source = jnp.concatenate([root[:dim].astype(BF16) for root in roots[1:]], 1)
    product = jnp.dot(
        target,
        target_columns(source, norm_rows(source, scale, False)),
        preferred_element_type=F32,
    )
    out_ref[...] = lax.dot_general(
        jnp.concatenate(weights, 1),
        jnp.exp2(product),
        (((1,), (1,)), ((), ())),
        preferred_element_type=F32,
        precision=lax.Precision.HIGHEST,
    )


def route_kernel(own_ref, ahead_ref, *out_refs):
    row_index = lax.axis_index("gy")
    for bit, out_ref in enumerate(out_refs):
        upper_side = (row_index >> bit) & 1 == 1

        @pl.when(upper_side)
        def _():
            out_ref[...] = own_ref[...]

        @pl.when(jnp.logical_not(upper_side))
        def _():
            out_ref[...] = ahead_ref[...]


def add_kernel(*refs):
    refs[-1][0] = functools.reduce(jnp.add, [ref[...] for ref in refs[:-1]])


def join_kernel(*refs):
    parts, out_ref = refs[:-1], refs[-1]
    start = 0
    for part in parts:
        out_ref[pl.ds(start, part.shape[0])] = part[...]
        start += part.shape[0]


def fall_kernel(near_ref, root_ref, spread_ref, out_ref):
    total = near_ref[...]
    for part in split3(root_ref[...]):
        total += jnp.dot(part, spread_ref[...], preferred_element_type=F32)
    out_ref[...] = total


def last_kernel(local_ref, *refs):
    total = local_ref[...]
    for ref in refs[:-1]:
        total += ref[...].astype(F32)
    refs[-1][...] = total


def shape(*dims, dtype=F32):
    return jax.ShapeDtypeStruct(dims, dtype)


def kept(*dims, dtype=F32):
    return pltpu.VMEM(dims, dtype)


def run(kernel, outs, *args, flops=2**20, memory=4, scratch=(), aliases=None):
    many = isinstance(outs, tuple)
    return pl.pallas_call(
        kernel,
        out_shape=outs,
        in_specs=[VMEM] * len(args),
        out_specs=(VMEM,) * len(outs) if many else VMEM,
        scratch_shapes=list(scratch),
        input_output_aliases=aliases or {},
        cost_estimate=pl.CostEstimate(flops=flops, bytes_accessed=2**16, transcendentals=0),
        compiler_params=pltpu.CompilerParams(vmem_limit_bytes=memory * 2**20),
    )(*[pltpu.with_memory_space_constraint(arg, pltpu.VMEM) for arg in args])


def landing(partner, back):
    reach, count = lax.axis_size("gy"), lax.axis_size("gx") * lax.axis_size("gy")
    pairs = []
    for source in range(count):
        row = source % reach
        step = ((row ^ partner) - row - 1) % reach + 1
        if source + step < count:
            pairs.append((source, source + step))
    return lax.ppermute(back, ("gx", "gy"), pairs)


def on_device(
    points,
    vectors,
    leaf_pick,
    leaf_assign,
    device_pick,
    device_assign,
    node_pick,
    node_assign,
    far_mask,
    near_lower,
    near_upper,
):
    dim, device_cols = points.shape
    cols = vectors.shape[0]
    leaf = device_cols // LPD
    scale = 2.0 * KERNEL_RATE / dim * LOG2E
    width = 3 * dim + ROWS_AUG
    gx_count, reach = lax.axis_size("gx"), lax.axis_size("gy")
    levels = reach.bit_length() - 1
    slots = near_lower.shape[2]
    group = next(size for size in range(12, 0, -1) if slots % size == 0)
    tile_flops = 2 * leaf * leaf * (256 + 2 * 256)
    block = kept(dim + cols, device_cols, dtype=BF16)
    root_shape = (dim + cols, SKEL)

    packed = jnp.concatenate([points, vectors], 0)
    ahead = passed_along(packed, "gx", -1)

    share, spread = run(
        functools.partial(rise_kernel, levels, leaf, dim),
        (kept(*root_shape), kept(SKEL, device_cols, dtype=BF16)),
        packed,
        leaf_pick,
        leaf_assign,
        device_pick,
        device_assign,
        jnp.transpose(node_pick, (1, 0, 2)),
        jnp.transpose(node_assign, (1, 0, 2)),
        flops=2**29,
        memory=6,
    )
    shares = [swapped(share, "gy", partner) for partner in range(1, reach)]
    own_root = run(add_kernel, kept(1, *root_shape), share, *shares)
    roots, sent = [own_root], own_root
    for bit in range(gx_count.bit_length() - 1):
        if bit:
            sent = run(join_kernel, kept(1 << bit, *root_shape), *roots)
        roots.append(swapped(sent, "gx", 1 << bit))

    rows, near = run(
        functools.partial(self_kernel, scale, leaf),
        (kept(device_cols, width, dtype=BF16), kept(cols, device_cols)),
        packed,
        flops=10 * tile_flops,
        memory=20,
        scratch=[
            pltpu.VMEM((ROWS_AUG, device_cols), BF16),
            pltpu.VMEM((LPD * (LPD + 1) // 2, leaf, leaf), BF16),
            pltpu.VMEM((LPD * (LPD + 1) // 2, leaf, leaf), BF16),
        ],
    )

    def meet(partner, other, near):
        return run(
            functools.partial(pair_kernel, scale, leaf, partner, group),
            (kept(cols, device_cols), kept(cols, device_cols, dtype=BF16)),
            near_lower,
            near_upper,
            rows,
            packed,
            other,
            near,
            flops=slots * tile_flops,
            memory=24,
            scratch=[
                pltpu.VMEM((ROWS_AUG, device_cols), BF16),
                pltpu.VMEM((cols, device_cols), F32),
                pltpu.VMEM((group, leaf, leaf), BF16),
                pltpu.VMEM((group, leaf, leaf), BF16),
            ],
            aliases={5: 0},
        )

    payloads = run(route_kernel, (block,) * levels, packed, ahead)
    others = {
        partner: swapped(payloads[partner.bit_length() - 1], "gy", partner)
        for partner in range(reach - 1, 0, -1)
    }
    near, upper = meet(0, ahead, near)
    landed = [passed_along(upper, "gx", 1)]
    for partner in range(reach - 1, 0, -1):
        near, upper = meet(partner, others[partner], near)
        landed.append(landing(partner, upper))
    root = run(
        functools.partial(root_kernel, scale), kept(cols, SKEL), far_mask, *roots, flops=2**28
    )
    local = run(fall_kernel, kept(cols, device_cols), near, root, spread, flops=2**26)
    return run(last_kernel, shape(cols, device_cols), local, *landed)


def solution(mesh):
    placed = (
        P(None, ("gx", "gy")),
        P(None, ("gx", "gy")),
        P(("gx", "gy"), None),
        P(("gx", "gy"), None),
        P(("gx", "gy"), None),
        P(("gx", "gy"), None),
        P("gx", None, None),
        P("gx", None, None),
        P("gx", None),
        P(("gx", "gy"), None, None),
        P(("gx", "gy"), None, None),
    )


    return jax.shard_map(
        on_device, mesh=mesh, in_specs=placed, out_specs=P(None, ("gx", "gy")), check_vma=False
    )
```
